32 devices in a mesh: tok: 8 (over z, y), feat: 4 (over x, core).
Axes of the slice: x: 2, y: 2, z: 4, core: 2. Of those that a mesh axis runs over, the one named last changes fastest.
Arguments:
- block_input: bfloat16 [4728, 1536], P('tok', 'feat'), may hold values from -6 to 6
- norm_gain1: float32 [768], P('feat'), may hold values from 0.5 to 1.5
- norm_shift1: float32 [768], P('feat'), may hold values from -3 to 3
- qkv_weight: bfloat16 [768, 3, 768], P('tok', None, 'feat'), may hold values from -1 to 1
- query_bias: float32 [768], P('feat'), may hold values from -3 to 3
- value_bias: float32 [768], P('feat'), may hold values from -3 to 3
- out_weight: bfloat16 [768, 768], P('feat', 'tok'), may hold values from -0.625 to 0.625
- out_bias: float32 [768], P('feat'), may hold values from -3 to 3
- norm_gain2: float32 [768], P('feat'), may hold values from 0.5 to 1.5
- norm_shift2: float32 [768], P('feat'), may hold values from -3 to 3
- up_weight: bfloat16 [768, 3072], P('tok', 'feat'), may hold values from -0.21875 to 0.21875
- up_bias: float32 [3072], P('feat'), may hold values from -3 to 3
- down_weight: bfloat16 [3072, 768], P('feat', 'tok'), may hold values from -0.109375 to 0.109375
- down_bias: float32 [768], P('feat'), may hold values from -3 to 3
- out_grad: bfloat16 [4728, 1536], P('tok', 'feat'), may hold values from -20 to 20
Outputs:
- block_output: bfloat16 [4728, 1536], P('tok', 'feat')
- input_grad: float32 [4728, 1536], P('tok', 'feat')
- grad_gain1: float32 [768], P('feat')
- grad_shift1: float32 [768], P('feat')
- grad_qkv: float32 [768, 3, 768], P('tok', None, 'feat')
- grad_qbias: float32 [768], P('feat')
- grad_vbias: float32 [768], P('feat')
- grad_wout: float32 [768, 768], P('feat', 'tok')
- grad_obias: float32 [768], P('feat')
- grad_gain2: float32 [768], P('feat')
- grad_shift2: float32 [768], P('feat')
- grad_wup: float32 [768, 3072], P('tok', 'feat')
- grad_upbias: float32 [3072], P('feat')
- grad_wdown: float32 [3072, 768], P('feat', 'tok')
- grad_dbias: float32 [768], P('feat')
The draws below stay inside these ranges and needn't reach their ends.
All inputs are finite; a program needn't handle non-finite values.
Results may differ from the reference program's by a relative error of at most 0.019.
Values may be sent and summed in bfloat16 or wider, within the bound.
No kernel may reach another device: no remote copies, remote signals or barrier semaphores. Data moves between devices by JAX's collectives and lax.ppermute only.
A program may use at most 128 MiB of HBM per device.

```python
import math
import jax
import jax.numpy as jnp
from jax import lax

D = 768
HEADS = 12
HD = 64
FF = 3072
SEQ = 197
TOKENS = 9456
N_TOK = 8
N_FEAT = 4


def pack_tokens(values):
    slice_width = D // N_FEAT
    return jnp.transpose(values.reshape(TOKENS // 2, 2, N_FEAT, slice_width), (0, 2, 1, 3)).reshape(TOKENS // 2, 2 * D)


def draw_block_input(key, part):
    first = jax.random.fold_in(jax.random.fold_in(key, 11), 0)
    values = jnp.clip(jax.random.normal(first, (TOKENS, D), jnp.float32), -6.0, 6.0)
    return pack_tokens(values).astype(jnp.bfloat16)


def draw_qkv_weight(key, part):
    values = jnp.clip(jax.random.normal(jax.random.fold_in(key, 13), (D, 3, D), jnp.float32), -6.0, 6.0) * D ** (-0.5)
    return values.astype(jnp.bfloat16)


def draw_out_grad(key, part):
    first = jax.random.fold_in(key, 0)
    positions = jnp.arange(TOKENS, dtype=jnp.float32)
    scale = jnp.exp(jnp.log(3.0) * positions / max(TOKENS - 1, 1))[:, None]
    values = jax.random.normal(first, (TOKENS, D), jnp.float32) * scale
    values = jnp.clip(values, -20.0, 20.0)
    return pack_tokens(values).astype(jnp.bfloat16)


def steps_of(own_key, shape, cuts, low, largest):
    level = 1.0
    for dim, blocks in cuts:
        heights = jax.random.uniform(jax.random.fold_in(jax.random.fold_in(own_key, 6), dim), (blocks,), jnp.float32, low / len(cuts), largest / len(cuts))
        level = level * jnp.repeat(jnp.exp(heights), shape[dim] // blocks).reshape((-1,) + (1,) * (len(shape) - 1 - dim))
    return level


def bell_draw(key, shape, width, bound, cuts=(), held_as=jnp.bfloat16):
    level = steps_of(key, shape, cuts, -0.22, 0.18) if cuts else 1.0
    result = jax.random.normal(key, shape, jnp.float32) * width * level
    return jnp.minimum(jnp.maximum(result, -bound), bound).astype(held_as)


def setup_inputs(seed: int = 0) -> dict:
    seeds = jax.random.split(jax.random.key(seed), 16)
    block_input = draw_block_input(jax.random.fold_in(seeds[15], 71), 0)
    norm_gain1 = jnp.clip(1.0 + 0.1 * jax.random.normal(seeds[1], (D,), jnp.float32), 0.5, 1.5)
    norm_shift1 = bell_draw(seeds[2], (D,), 0.5, 3.0, ((0, 4),), jnp.float32)
    qkv_weight = draw_qkv_weight(jax.random.fold_in(seeds[15], 71), 0)
    query_bias = bell_draw(seeds[4], (D,), 0.5, 3.0, ((0, 4),), jnp.float32)
    value_bias = bell_draw(seeds[5], (D,), 0.5, 3.0, ((0, 4),), jnp.float32)
    out_weight = bell_draw(seeds[6], (D, D), (D // 8) ** -0.5, 0.625, ((0, 4), (1, 8)))
    out_bias = bell_draw(seeds[7], (D,), 0.5, 3.0, ((0, 4),), jnp.float32)
    norm_gain2 = jnp.clip(1.0 + 0.1 * jax.random.normal(seeds[8], (D,), jnp.float32), 0.5, 1.5)
    norm_shift2 = bell_draw(seeds[9], (D,), 0.5, 3.0, ((0, 4),), jnp.float32)
    up_weight = bell_draw(seeds[10], (D, FF), D ** -0.5, 0.21875, ((0, 8), (1, 4)))
    up_bias = bell_draw(seeds[11], (FF,), 0.5, 3.0, ((0, 4),), jnp.float32)
    down_weight = bell_draw(seeds[12], (FF, D), FF ** -0.5, 0.109375, ((0, 4), (1, 8)))
    down_bias = bell_draw(seeds[13], (D,), 0.5, 3.0, ((0, 4),), jnp.float32)
    out_grad = draw_out_grad(jax.random.fold_in(seeds[15], 71), 0)
    return dict(block_input=block_input, norm_gain1=norm_gain1, norm_shift1=norm_shift1, qkv_weight=qkv_weight, query_bias=query_bias, value_bias=value_bias, out_weight=out_weight, out_bias=out_bias, norm_gain2=norm_gain2, norm_shift2=norm_shift2, up_weight=up_weight, up_bias=up_bias, down_weight=down_weight, down_bias=down_bias, out_grad=out_grad)


HALF_ROOT = 0.7071067811865476
INV_ROOT_TWO_PI = 0.3989422804014327
EPSILON = 1e-06

def unpack_rows(packed):
    slice_width = D // N_FEAT
    return jnp.transpose(packed.reshape(TOKENS // 2, N_FEAT, 2, slice_width), (0, 2, 1, 3)).reshape(TOKENS, D)

def pack_rows(values):
    slice_width = D // N_FEAT
    return jnp.transpose(values.reshape(TOKENS // 2, 2, N_FEAT, slice_width), (0, 2, 1, 3)).reshape(TOKENS // 2, 2 * D)

def gelu_value(values):
    return 0.5 * values * (1.0 + lax.erf(values * HALF_ROOT))

def gelu_slope(values):
    return 0.5 * (1.0 + lax.erf(values * HALF_ROOT)) + values * jnp.exp(-0.5 * values * values) * INV_ROOT_TWO_PI

def product(left, right):
    return jnp.dot(left, right, preferred_element_type=jnp.float32)

def normalize(values, gain, shift):
    mean_val = lax.optimization_barrier(jnp.mean(values, axis=1, keepdims=True))
    variance = lax.optimization_barrier(jnp.mean(values * values, axis=1, keepdims=True)) - mean_val * mean_val
    inv_std = lax.rsqrt(variance + EPSILON)
    centered = (values - mean_val) * inv_std
    return (centered, inv_std, (centered * gain + shift).astype(jnp.bfloat16))

def norm_back(d_norm, centered, inv_std, gain):
    scaled = d_norm * gain
    first = lax.optimization_barrier(jnp.mean(scaled, axis=1, keepdims=True))
    second = lax.optimization_barrier(jnp.mean(scaled * centered, axis=1, keepdims=True))
    return (inv_std * (scaled - first - centered * second), lax.optimization_barrier(jnp.sum(d_norm * centered, axis=0)), lax.optimization_barrier(jnp.sum(d_norm, axis=0)))

def shaped(values):
    return values.reshape(-1, SEQ, HEADS, HD).astype(jnp.float32)

def attend(query, keys_rows, values):
    scale = 1.0 / math.sqrt(HD)
    scores = jnp.einsum('bqhd,bkhd->bhqk', shaped(query), shaped(keys_rows)) * scale
    log_total = jax.nn.logsumexp(scores, axis=-1)
    probs = jnp.exp(scores - log_total[..., None]).astype(jnp.bfloat16)
    probs = lax.optimization_barrier(probs).astype(jnp.float32)
    attended = jnp.einsum('bhqk,bkhd->bqhd', probs, shaped(values))
    return (attended.reshape(-1, D).astype(jnp.bfloat16), log_total)

def attend_back(query, keys_rows, values, attended, log_total, d_att):
    scale = 1.0 / math.sqrt(HD)
    scores = jnp.einsum('bqhd,bkhd->bhqk', shaped(query), shaped(keys_rows)) * scale
    probs_full = jnp.exp(scores - log_total[..., None])
    probs = lax.optimization_barrier(probs_full.astype(jnp.bfloat16)).astype(jnp.float32)
    d_shaped = shaped(d_att)
    d_values = jnp.einsum('bhqk,bqhd->bkhd', probs, d_shaped)
    d_probs = jnp.einsum('bqhd,bkhd->bhqk', d_shaped, shaped(values))
    delta = jnp.transpose(lax.optimization_barrier(jnp.sum(d_shaped * shaped(attended), axis=-1)), (0, 2, 1))
    d_scores = (probs_full * (d_probs - delta[..., None]) * scale).astype(jnp.bfloat16)
    d_scores = lax.optimization_barrier(d_scores).astype(jnp.float32)
    d_query = jnp.einsum('bhqk,bkhd->bqhd', d_scores, shaped(keys_rows))
    d_keys = jnp.einsum('bhqk,bqhd->bkhd', d_scores, shaped(query))
    return (d_query.reshape(-1, D), d_keys.reshape(-1, D), d_values.reshape(-1, D))

def reference(block_input, norm_gain1, norm_shift1, qkv_weight, query_bias, value_bias, out_weight, out_bias, norm_gain2, norm_shift2, up_weight, up_bias, down_weight, down_bias, out_grad):

    def one_block(carry, pair):
        inputs, grads = pair
        inputs32 = inputs.astype(jnp.float32)
        centered1, inv_std1, normed1 = normalize(inputs32, norm_gain1, norm_shift1)
        query = (product(normed1, qkv_weight[:, 0, :]) + query_bias).astype(jnp.bfloat16)
        keys_rows = product(normed1, qkv_weight[:, 1, :]).astype(jnp.bfloat16)
        values = (product(normed1, qkv_weight[:, 2, :]) + value_bias).astype(jnp.bfloat16)
        attended, log_total = attend(query, keys_rows, values)
        residual = inputs32 + product(attended, out_weight) + out_bias
        centered2, inv_std2, normed2 = normalize(residual, norm_gain2, norm_shift2)
        before = product(normed2, up_weight) + up_bias
        hidden = gelu_value(before).astype(jnp.bfloat16)
        output = (residual + product(hidden, down_weight) + down_bias).astype(jnp.bfloat16)
        grad32 = grads.astype(jnp.float32)
        grad_wdown = product(hidden.T, grads)
        d_before = product(grads, down_weight.T) * gelu_slope(before)
        d_before_b = d_before.astype(jnp.bfloat16)
        grad_wup = product(normed2.T, d_before_b)
        d_normed2 = product(d_before_b, up_weight.T)
        d_resid_ln, grad_gain2, grad_shift2 = norm_back(d_normed2, centered2, inv_std2, norm_gain2)
        d_resid = grad32 + d_resid_ln
        d_resid_b = d_resid.astype(jnp.bfloat16)
        grad_wout = product(attended.T, d_resid_b)
        d_att = product(d_resid_b, out_weight.T).astype(jnp.bfloat16)
        d_query, d_keys, d_values = attend_back(query, keys_rows, values, attended, log_total, d_att)
        d_qkv = jnp.stack([d_query, d_keys, d_values], axis=1).astype(jnp.bfloat16)
        grad_qkv = jnp.stack([product(normed1.T, d_qkv[:, which]) for which in range(3)], axis=1)
        d_normed1 = product(d_qkv[:, 0], qkv_weight[:, 0].T) + product(d_qkv[:, 1], qkv_weight[:, 1].T) + product(d_qkv[:, 2], qkv_weight[:, 2].T)
        d_in_ln, grad_gain1, grad_shift1 = norm_back(d_normed1, centered1, inv_std1, norm_gain1)
        input_grad = d_resid + d_in_ln
        update = (grad_gain1, grad_shift1, grad_qkv, lax.optimization_barrier(jnp.sum(d_query, axis=0)), lax.optimization_barrier(jnp.sum(d_values, axis=0)), grad_wout, lax.optimization_barrier(jnp.sum(d_resid, axis=0)), grad_gain2, grad_shift2, grad_wup, lax.optimization_barrier(jnp.sum(d_before, axis=0)), grad_wdown, lax.optimization_barrier(jnp.sum(grad32, axis=0)))
        carry = jax.tree.map(lambda total, part: total + part, carry, update)
        return (carry, (output, input_grad))
    zeros_d = jnp.zeros((D,), jnp.float32)
    start = (zeros_d, zeros_d, jnp.zeros((D, 3, D), jnp.float32), zeros_d, zeros_d, jnp.zeros((D, D), jnp.float32), zeros_d, zeros_d, zeros_d, jnp.zeros((D, FF), jnp.float32), jnp.zeros((FF,), jnp.float32), jnp.zeros((FF, D), jnp.float32), zeros_d)
    blocks_in = unpack_rows(block_input).reshape(N_TOK, -1, D)
    blocks_grad = unpack_rows(out_grad).reshape(N_TOK, -1, D)
    totals, (outputs, input_grads) = lax.scan(one_block, start, (blocks_in, blocks_grad))
    return (pack_rows(outputs.reshape(TOKENS, D)), pack_rows(input_grads.reshape(TOKENS, D)), totals[0], totals[1], totals[2], totals[3], totals[4], totals[5], totals[6], totals[7], totals[8], totals[9], totals[10], totals[11], totals[12])
```

```python
import math

import jax
import jax.numpy as jnp
from jax import lax
from jax.experimental import pallas as pl
from jax.experimental.pallas import tpu as pltpu
from jax.sharding import PartitionSpec as P

HD = 64
SEQ = 197
PAD = 208
HALF_ROOT = 0.7071067811865476
INV_ROOT_TWO_PI = 0.3989422804014327
EPSILON = 1e-06
BF = jnp.bfloat16
F32 = jnp.float32


def dot_nn(left, right):
    return lax.dot_general(left, right, (((1,), (0,)), ((), ())), preferred_element_type=F32)


def dot_nt(left, right):
    return lax.dot_general(left, right, (((1,), (1,)), ((), ())), preferred_element_type=F32)


def dot_tn(left, right):
    return lax.dot_general(left, right, (((0,), (0,)), ((), ())), preferred_element_type=F32)


def swap(values, axis, bit):
    size = lax.axis_size(axis)
    return lax.ppermute(values, axis, [(i, i ^ bit) for i in range(size)])


def swap_x(values):
    return swap(values, "feat", 2)


def swap_core(values):
    return swap(values, "feat", 1)


def in_order(bit, own, other, axis):
    low = jnp.where(bit == 0, own, other)
    high = jnp.where(bit == 0, other, own)
    return jnp.stack([low, high], axis=axis)


def tok_bits():
    return int(math.log2(lax.axis_size("tok")))


def gather_outer(values, tok):
    for k in range(1, tok_bits()):
        values = in_order((tok >> k) & 1, values, swap(values, "tok", 1 << k), 0)
    return values


def gather_inner(values, tok, lead):
    return in_order(tok & 1, values, swap(values, "tok", 1), lead + tok_bits() - 1)


def flat_rows(values, lead):
    shape = values.shape
    return values.reshape(shape[:lead] + (-1, shape[-1]))


def gather_tok_then_x(values, tok):
    own = flat_rows(gather_inner(values, tok, 0), 0)
    return own, swap_x(own)


def gather_x_then_tok(values, tok):
    pair = jnp.stack([values, swap_x(values)])
    both = flat_rows(gather_inner(pair, tok, 1), 1)
    return both[0], both[1]


def scatter_outer(values, tok):
    for k in range(tok_bits() - 1, 0, -1):
        bit = (tok >> k) & 1
        kept = lax.dynamic_index_in_dim(values, bit, 0, keepdims=False)
        sent = lax.dynamic_index_in_dim(values, 1 - bit, 0, keepdims=False)
        values = kept.astype(F32) + swap(sent, "tok", 1 << k).astype(F32)
        if k > 1:
            values = values.astype(BF)
    return values


def scatter_inner(values, tok, axis):
    bit = tok & 1
    kept = lax.dynamic_index_in_dim(values, bit, axis, keepdims=False)
    sent = lax.dynamic_index_in_dim(values, 1 - bit, axis, keepdims=False)
    return (kept.astype(F32) + swap(sent, "tok", 1).astype(F32)).astype(BF)


def split_tok(values):
    bits = tok_bits()
    rows = values.shape[0] // (1 << bits)
    return values.reshape((2,) * bits + (rows, values.shape[1]))


def scatter_x_then_tok(own, other, tok):
    total = (own.astype(F32) + swap_x(other).astype(F32)).astype(BF)
    total = split_tok(total)
    return scatter_outer(scatter_inner(total, tok, tok_bits() - 1), tok)


def scatter_tok_then_x(own, other, tok):
    pair = jnp.stack([split_tok(own), split_tok(other)])
    pair = scatter_inner(pair, tok, tok_bits())
    total = (pair[0].astype(F32) + swap_x(pair[1]).astype(F32)).astype(BF)
    return scatter_outer(total, tok)


def attend_kernel(x_ref, h1_ref, h2_ref, qb_ref, vb_ref, q_ref, k_ref, v_ref, att_ref, p_ref, out_ref):
    x = x_ref[...]
    width = 3 * HD
    lane = lax.broadcasted_iota(jnp.int32, (PAD, width), 1)
    col = lax.broadcasted_iota(jnp.int32, (PAD, PAD), 1)
    total = jnp.zeros((PAD, x.shape[1]), F32)
    for r in range(2):
        qk = dot_nn(x, h1_ref[r])
        q = (qk[:, :width] + qb_ref[r]).astype(BF)
        k = qk[:, width:].astype(BF)
        v = (dot_nn(x, h2_ref[r, :, :width]) + vb_ref[r]).astype(BF)
        q_ref[r] = q
        k_ref[r] = k
        v_ref[r] = v
        acc = jnp.zeros((PAD, width), F32)
        for h in range(3):
            mine = (lane >= h * HD) & (lane < (h + 1) * HD)
            qh = jnp.where(mine, q, jnp.zeros_like(q))
            s = dot_nt(qh, k) * (1.0 / math.sqrt(HD))
            s = jnp.where(col < SEQ, s, -1e30)
            e = jnp.exp(s - jnp.max(s, axis=1, keepdims=True))
            p = (e / jnp.sum(e, axis=1, keepdims=True)).astype(BF)
            p_ref[r * 3 + h] = p
            acc = jnp.where(mine, dot_nn(p, v), acc)
        att = acc.astype(BF)
        att_ref[r] = att
        total = total + dot_nt(att, h2_ref[r, :, width:])
    out_ref[...] = total.astype(BF)


def attend(normed, h1, h2, qb, vb):
    rows, dim = normed.shape
    images = rows // PAD
    width = 3 * HD
    full = lambda *shape: pl.BlockSpec(shape, lambda i: (0,) * len(shape))
    act = pl.BlockSpec((2, PAD, width), lambda i: (0, i, 0))
    act_shape = jax.ShapeDtypeStruct((2, rows, width), BF)
    return pl.pallas_call(
        attend_kernel,
        grid=(images,),
        in_specs=[
            pl.BlockSpec((PAD, dim), lambda i: (i, 0)),
            full(2, dim, 2 * width),
            full(2, dim, 2 * width),
            full(2, 1, width),
            full(2, 1, width),
        ],
        out_specs=[
            act,
            act,
            act,
            act,
            pl.BlockSpec((6, PAD, PAD), lambda i: (i, 0, 0)),
            pl.BlockSpec((PAD, dim), lambda i: (i, 0)),
        ],
        out_shape=[
            act_shape,
            act_shape,
            act_shape,
            act_shape,
            jax.ShapeDtypeStruct((6 * images, PAD, PAD), BF),
            jax.ShapeDtypeStruct((rows, dim), BF),
        ],
        name="attend",
    )(normed, h1, h2, qb, vb)


def attend_back_kernel(
    g_ref, q_ref, k_ref, v_ref, att_ref, p_ref, h1_ref, h2_ref, dqkv_ref, out_ref, qs_ref, vs_ref
):
    g = g_ref[...]
    width = 3 * HD
    scale = 1.0 / math.sqrt(HD)
    lane = lax.broadcasted_iota(jnp.int32, (PAD, width), 1)
    total = jnp.zeros((PAD, g.shape[1]), F32)

    @pl.when(pl.program_id(0) == 0)
    def _():
        qs_ref[...] = jnp.zeros_like(qs_ref)
        vs_ref[...] = jnp.zeros_like(vs_ref)

    for r in range(2):
        d_att = dot_nn(g, h2_ref[r, :, width:]).astype(BF)
        q, k, v = q_ref[r], k_ref[r], v_ref[r]
        crossed = d_att.astype(F32) * att_ref[r].astype(F32)
        dq = jnp.zeros((PAD, width), F32)
        dk = jnp.zeros((PAD, width), F32)
        dv = jnp.zeros((PAD, width), F32)
        for h in range(3):
            mine = (lane >= h * HD) & (lane < (h + 1) * HD)
            p = p_ref[r * 3 + h]
            gh = jnp.where(mine, d_att, jnp.zeros_like(d_att))
            delta = jnp.sum(jnp.where(mine, crossed, 0.0), axis=1, keepdims=True)
            dp = dot_nt(gh, v)
            ds = (p.astype(F32) * (dp - delta) * scale).astype(BF)
            dv = jnp.where(mine, dot_tn(p, d_att), dv)
            dq = jnp.where(mine, dot_nn(ds, k), dq)
            dk = jnp.where(mine, dot_tn(ds, q), dk)
        qs_ref[r] += jnp.sum(dq, axis=0, keepdims=True)
        vs_ref[r] += jnp.sum(dv, axis=0, keepdims=True)
        dq, dk, dv = dq.astype(BF), dk.astype(BF), dv.astype(BF)
        dqkv_ref[r] = jnp.concatenate([dq, dk, dv], axis=1)
        total = total + dot_nt(dq, h1_ref[r, :, :width]) + dot_nt(dk, h1_ref[r, :, width:])
        total = total + dot_nt(dv, h2_ref[r, :, :width])
    out_ref[...] = total.astype(BF)


def attend_back(grad, q, k, v, att, p, h1, h2):
    rows, dim = grad.shape
    images = rows // PAD
    width = 3 * HD
    full = lambda *shape: pl.BlockSpec(shape, lambda i: (0,) * len(shape))
    act = pl.BlockSpec((2, PAD, width), lambda i: (0, i, 0))
    return pl.pallas_call(
        attend_back_kernel,
        grid=(images,),
        in_specs=[
            pl.BlockSpec((PAD, dim), lambda i: (i, 0)),
            act,
            act,
            act,
            act,
            pl.BlockSpec((6, PAD, PAD), lambda i: (i, 0, 0)),
            full(2, dim, 2 * width),
            full(2, dim, 2 * width),
        ],
        out_specs=[
            pl.BlockSpec((2, PAD, 3 * width), lambda i: (0, i, 0)),
            pl.BlockSpec((PAD, dim), lambda i: (i, 0)),
            full(2, 1, width),
            full(2, 1, width),
        ],
        out_shape=[
            jax.ShapeDtypeStruct((2, rows, 3 * width), BF),
            jax.ShapeDtypeStruct((rows, dim), BF),
            jax.ShapeDtypeStruct((2, 1, width), F32),
            jax.ShapeDtypeStruct((2, 1, width), F32),
        ],
        name="attend_back",
    )(grad, q, k, v, att, p, h1, h2)


def normalize(values, gain, shift):
    mean_val = jnp.mean(values, axis=1, keepdims=True)
    variance = jnp.mean(values * values, axis=1, keepdims=True) - mean_val * mean_val
    inv_std = lax.rsqrt(variance + EPSILON)
    centered = (values - mean_val) * inv_std
    return centered, inv_std, (centered * gain + shift).astype(BF)


def norm_back(d_norm, centered, inv_std, gain):
    scaled = d_norm * gain
    first = jnp.mean(scaled, axis=1, keepdims=True)
    second = jnp.mean(scaled * centered, axis=1, keepdims=True)
    return (
        inv_std * (scaled - first - centered * second),
        jnp.sum(d_norm * centered, axis=0),
        jnp.sum(d_norm, axis=0),
    )


def body(
    block_input,
    norm_gain1,
    norm_shift1,
    qkv_weight,
    query_bias,
    value_bias,
    out_weight,
    out_bias,
    norm_gain2,
    norm_shift2,
    up_weight,
    up_bias,
    down_weight,
    down_bias,
    out_grad,
):
    feat = lax.axis_index("feat")
    tok = lax.axis_index("tok")
    x, core = feat // 2, feat % 2
    rows = block_input.shape[0]
    local = block_input.shape[1] // 2
    dim = local * lax.axis_size("feat")
    hidden_w = up_weight.shape[1]
    part = (rows + 1) // 2
    shift_rows = rows - part
    half_tokens = rows
    images = half_tokens // SEQ
    first_token = x * half_tokens - 2 * x * shift_rows

    def own_tokens(values):
        own = lax.dynamic_slice_in_dim(values, x * shift_rows, part, 0)
        sent = lax.dynamic_slice_in_dim(values, (1 - x) * shift_rows, part, 0)
        pair = jnp.stack([own, swap_x(sent)])
        other = swap_core(pair)
        by_core = jnp.stack([jnp.where(core == 0, pair, other), jnp.where(core == 0, other, pair)])
        by_x = jnp.stack(
            [
                jnp.where(x == 0, by_core[:, 0], by_core[:, 1]),
                jnp.where(x == 0, by_core[:, 1], by_core[:, 0]),
            ]
        )
        even = [by_x[f // 2, f % 2][:, :local] for f in range(4)]
        odd = [by_x[f // 2, f % 2][:, local:] for f in range(4)]
        return jnp.concatenate(
            [jnp.concatenate(even, axis=1), jnp.concatenate(odd, axis=1)], axis=0
        )

    slot = lax.broadcasted_iota(jnp.int32, (images * PAD, 2 * part), 0)
    source = lax.broadcasted_iota(jnp.int32, (images * PAD, 2 * part), 1)
    place = slot % PAD
    token = first_token + (slot // PAD) * SEQ + place
    hit = (place < SEQ) & (source == (token % 2) * part + token // 2)
    select = jnp.where(hit, 1.0, 0.0).astype(BF)

    own_small = jnp.concatenate(
        [norm_gain1, norm_shift1, norm_gain2, norm_shift2, out_bias, down_bias]
        + [query_bias, value_bias, up_bias]
    ).reshape(-1, 128)
    far_small = swap_x(own_small)
    pair_small = jnp.stack([own_small.reshape(-1), far_small.reshape(-1)])
    qb = pair_small[:, 6 * local : 7 * local].reshape(2, 1, local)
    vb = pair_small[:, 7 * local : 8 * local].reshape(2, 1, local)
    upb = pair_small[:, 8 * local :]
    wide = pair_small[:, : 6 * local].reshape(2, -1, 128)
    wide_other = swap_core(wide)
    by_core = jnp.stack([jnp.where(core == 0, wide, wide_other), jnp.where(core == 0, wide_other, wide)])
    by_x = jnp.stack(
        [
            jnp.where(x == 0, by_core[:, 0], by_core[:, 1]),
            jnp.where(x == 0, by_core[:, 1], by_core[:, 0]),
        ]
    )
    vectors = by_x.reshape(4, 6, local).transpose(1, 0, 2).reshape(6, dim)
    gain1, shift1, gain2, shift2, obias, dbias = [vectors[i][None] for i in range(6)]

    a_local = jnp.concatenate([qkv_weight.reshape(-1, 3 * local), out_weight.T], axis=1)
    a_pair = jnp.stack([a_local[:, : 2 * local], a_local[:, 2 * local :]])
    b_local = up_weight
    c_local = down_weight.T

    bi = own_tokens(block_input)

    bits = tok_bits()
    a_half = a_pair
    for k in range(1, bits):
        a_half = in_order((tok >> k) & 1, a_half, swap(a_half, "tok", 1 << k), 1)
    h1_own, h1_far = gather_tok_then_x(a_half[0], tok)
    h2_own, h2_far = gather_x_then_tok(a_half[1], tok)
    h1 = jnp.stack([h1_own, h1_far])
    h2 = jnp.stack([h2_own, h2_far])
    up_own, up_far = gather_x_then_tok(gather_outer(b_local, tok), tok)
    down_own, down_far = gather_tok_then_x(gather_outer(c_local, tok), tok)
    og = own_tokens(out_grad)

    values = dot_nn(select, bi)
    grads = dot_nn(select, og)
    centered1, inv_std1, normed1 = normalize(values, gain1, shift1)
    q, k, v, att, probs, mixed = attend(normed1, h1, h2, qb, vb)
    residual = values + (mixed.astype(F32) + swap_core(mixed).astype(F32)) + obias
    centered2, inv_std2, normed2 = normalize(residual, gain2, shift2)
    grads_b = grads.astype(BF)

    def gelu_parts(weights, bias):
        before = dot_nn(normed2, weights) + bias
        cdf = 0.5 * (1.0 + lax.erf(before * HALF_ROOT))
        hidden = (before * cdf).astype(BF)
        slope = cdf + before * jnp.exp(-0.5 * before * before) * INV_ROOT_TWO_PI
        return hidden, slope

    hidden_own, slope_own = gelu_parts(up_own, upb[0])
    hidden_far, slope_far = gelu_parts(up_far, upb[1])
    d_before_own = dot_nn(grads_b, down_own) * slope_own
    d_before_far = dot_nn(grads_b, down_far) * slope_far
    db_own, db_far = d_before_own.astype(BF), d_before_far.astype(BF)
    dn2 = (dot_nt(db_own, up_own) + dot_nt(db_far, up_far)).astype(BF)
    dn2_other = swap_core(dn2)
    gc_own = dot_tn(grads_b, hidden_own).astype(BF)
    gc_far = dot_tn(grads_b, hidden_far).astype(BF)
    gb_own = dot_tn(normed2, db_own).astype(BF)
    gb_far = dot_tn(normed2, db_far).astype(BF)
    down_out = dot_nt(hidden_own, down_own) + dot_nt(hidden_far, down_far)

    grad_down = scatter_x_then_tok(gc_own, gc_far, tok)
    grad_up = scatter_tok_then_x(gb_own, gb_far, tok)

    def core_columns(values, which):
        cols = values.reshape(-1, 2, 2, local)
        return lax.dynamic_index_in_dim(cols, which, 2, keepdims=False).reshape(-1, 2 * local)

    def give_back(columns):
        packed = dot_tn(select, columns.astype(BF))
        even, odd = packed[:part], packed[part:]
        piece = [
            jnp.concatenate(
                [even[:, i * local : (i + 1) * local], odd[:, i * local : (i + 1) * local]], axis=1
            ).astype(BF)
            for i in range(2)
        ]
        own = jnp.where(x == 0, piece[0], piece[1])
        got = swap_x(jnp.where(x == 0, piece[1], piece[0]))
        low = jnp.where(x == 0, own, got).astype(F32)
        high = jnp.where(x == 0, got, own).astype(F32)
        return jnp.pad(low, ((0, shift_rows), (0, 0))) + jnp.pad(high, ((shift_rows, 0), (0, 0)))

    part_out = core_columns(down_out, core) + swap_core(
        core_columns(down_out, 1 - core).astype(BF)
    ).astype(F32)
    out_cols = core_columns(residual + dbias, core) + part_out
    block_output = give_back(out_cols).astype(BF)

    d_normed2 = dn2.astype(F32) + dn2_other.astype(F32)
    d_resid_ln, g_gain2, g_shift2 = norm_back(d_normed2, centered2, inv_std2, gain2)
    d_resid = grads + d_resid_ln
    d_resid_b = d_resid.astype(BF)
    d_qkv, dn1, q_sum, v_sum = attend_back(d_resid_b, q, k, v, att, probs, h1, h2)
    dn1_other = swap_core(dn1)
    ga = [
        jnp.concatenate([dot_tn(normed1, d_qkv[r]), dot_tn(d_resid_b, att[r])], axis=1).astype(BF)
        for r in range(2)
    ]
    ga1 = scatter_x_then_tok(ga[0][:, : 2 * local], ga[1][:, : 2 * local], tok)
    ga2 = scatter_tok_then_x(ga[0][:, 2 * local :], ga[1][:, 2 * local :], tok)
    d_normed1 = dn1.astype(F32) + dn1_other.astype(F32)
    d_in_ln, g_gain1, g_shift1 = norm_back(d_normed1, centered1, inv_std1, gain1)
    input_grad = give_back(core_columns(d_resid + d_in_ln, core))

    vecs = jnp.stack(
        [g_gain1, g_shift1, g_gain2, g_shift2, jnp.sum(d_resid, axis=0), jnp.sum(grads, axis=0)]
    ).reshape(6, 2, 2, local)
    vecs = lax.dynamic_index_in_dim(vecs, core, 2, keepdims=False)
    vec_own = lax.dynamic_index_in_dim(vecs, x, 1, keepdims=False).reshape(-1)
    vec_far = lax.dynamic_index_in_dim(vecs, 1 - x, 1, keepdims=False).reshape(-1)
    small_own = jnp.concatenate(
        [vec_own, q_sum[0, 0], v_sum[0, 0], jnp.sum(d_before_own, axis=0)]
    ).reshape(-1, 128)
    small_far = jnp.concatenate(
        [vec_far, q_sum[1, 0], v_sum[1, 0], jnp.sum(d_before_far, axis=0)]
    ).reshape(-1, 128)
    small = small_own + swap_x(small_far)
    for k in range(bits):
        small = small + swap(small, "tok", 1 << k)
    small = small.reshape(-1)
    cut = lambda i: small[i * local : (i + 1) * local]

    grad_a = jnp.concatenate([ga1, ga2], axis=1)
    return (
        block_output,
        input_grad,
        cut(0),
        cut(1),
        grad_a[:, : 3 * local].reshape(qkv_weight.shape),
        cut(6),
        cut(7),
        grad_a[:, 3 * local :].T,
        cut(4),
        cut(2),
        cut(3),
        grad_up,
        small[8 * local :],
        grad_down.T,
        cut(5),
    )


def solution(mesh):
    in_specs = (
        P("tok", "feat"),
        P("feat"),
        P("feat"),
        P("tok", None, "feat"),
        P("feat"),
        P("feat"),
        P("feat", "tok"),
        P("feat"),
        P("feat"),
        P("feat"),
        P("tok", "feat"),
        P("feat"),
        P("feat", "tok"),
        P("feat"),
        P("tok", "feat"),
    )
    out_specs = (
        P("tok", "feat"),
        P("tok", "feat"),
        P("feat"),
        P("feat"),
        P("tok", None, "feat"),
        P("feat"),
        P("feat"),
        P("feat", "tok"),
        P("feat"),
        P("feat"),
        P("feat"),
        P("tok", "feat"),
        P("feat"),
        P("feat", "tok"),
        P("feat"),
    )
    return jax.shard_map(body, mesh=mesh, in_specs=in_specs, out_specs=out_specs, check_vma=False)
```

```python
import math

import jax
import jax.numpy as jnp
from jax import lax
from jax.experimental import pallas as pl
from jax.experimental.pallas import tpu as pltpu
from jax.sharding import PartitionSpec as P

HD = 64
SEQ = 197
PAD = 208
HEADS = 3
WIDTH = HEADS * HD
EDGE = 384
HALF_ROOT = 0.7071067811865476
INV_ROOT_TWO_PI = 0.3989422804014327
EPSILON = 1e-06
BF = jnp.bfloat16
F32 = jnp.float32


def dot_nn(left, right):
    return lax.dot_general(left, right, (((1,), (0,)), ((), ())), preferred_element_type=F32)


def dot_nt(left, right):
    return lax.dot_general(left, right, (((1,), (1,)), ((), ())), preferred_element_type=F32)


def dot_tn(left, right):
    return lax.dot_general(left, right, (((0,), (0,)), ((), ())), preferred_element_type=F32)


def swap(values, axis, bit):
    size = lax.axis_size(axis)
    return lax.ppermute(values, axis, [(i, i ^ bit) for i in range(size)])


def swap_x(values):
    return swap(values, "feat", 2)


def swap_core(values):
    return swap(values, "feat", 1)


def swap_y(values):
    return swap(values, "tok", 1)


def after(value, *others):
    return lax.optimization_barrier((value,) + others)[0]


def tok_bits():
    return int(math.log2(lax.axis_size("tok")))


def outer_bits():
    return range(tok_bits() - 1, 0, -1)


def add_rows(kept, got):
    return kept.astype(F32) + got.astype(F32)


def scatter_outer(total):
    for k in reversed(outer_bits()):
        half = total.shape[0] // 2
        kept, sent = total[:half], total[half:]
        total = add_rows(kept, swap(sent.astype(BF), "tok", 1 << k))
    return total


def whole(*shape):
    return pl.BlockSpec(shape, lambda i: (0,) * len(shape))


def row_block(width):
    return pl.BlockSpec((PAD, width), lambda i: (i, 0))


def place(own_ref, far_ref, scratch):
    part = own_ref.shape[1]
    scratch[...] = jnp.zeros_like(scratch)
    for piece in range(4):
        rows = (own_ref if piece < 2 else far_ref)[piece % 2]
        for t in range(2):
            scratch[t, 0:part, piece * WIDTH : (piece + 1) * WIDTH] = rows[:, t * WIDTH : (t + 1) * WIDTH]


def tokens_kernel(own_ref, far_ref, select_ref, order_ref, out_ref, scratch):
    @pl.when(pl.program_id(0) == 0)
    def _():
        place(own_ref, far_ref, scratch)

    rows = dot_nn(select_ref[0], scratch[0]) + dot_nn(select_ref[1], scratch[1])
    out_ref[...] = dot_nn(rows.astype(BF), order_ref[...]).astype(BF)


def tokens_norm_kernel(own_ref, far_ref, select_ref, order_ref, gain_ref, shift_ref, out_ref, norm_ref, scratch):
    @pl.when(pl.program_id(0) == 0)
    def _():
        place(own_ref, far_ref, scratch)

    rows = dot_nn(select_ref[0], scratch[0]) + dot_nn(select_ref[1], scratch[1])
    values = dot_nn(rows.astype(BF), order_ref[...])
    out_ref[...] = values.astype(BF)
    centered, _ = center(values)
    norm_ref[...] = (centered * gain_ref[...] + shift_ref[...]).astype(BF)


def tokens(own, far, select, order, gain=None, shift=None):
    part, dim = own.shape[1], order.shape[0]
    rows = select.shape[1]
    normed = gain is not None
    vec = [gain, shift] if normed else []
    count = 2 if normed else 1
    return pl.pallas_call(
        tokens_norm_kernel if normed else tokens_kernel,
        grid=(rows // PAD,),
        in_specs=[
            whole(2, part, 2 * WIDTH),
            whole(2, part, 2 * WIDTH),
            pl.BlockSpec((2, PAD, EDGE), lambda i: (0, i, 0)),
            whole(dim, dim),
        ]
        + [whole(1, dim)] * len(vec),
        out_specs=[row_block(dim)] * count,
        out_shape=[jax.ShapeDtypeStruct((rows, dim), BF)] * count,
        scratch_shapes=[pltpu.VMEM((2, EDGE, dim), BF)],
        name="tokens_norm" if normed else "tokens",
    )(own, far, select, order, *vec)


def center(values):
    mean_val = jnp.mean(values, axis=1, keepdims=True)
    variance = jnp.mean(values * values, axis=1, keepdims=True) - mean_val * mean_val
    inv_std = lax.rsqrt(variance + EPSILON)
    return (values - mean_val) * inv_std, inv_std


def attend_kernel(x_ref, h1_ref, h2_ref, qb_ref, vb_ref, q_ref, k_ref, v_ref, att_ref, p_ref, out_ref):
    x = x_ref[...]
    lane = lax.broadcasted_iota(jnp.int32, (PAD, 256), 1)
    row = lax.broadcasted_iota(jnp.int32, (PAD, 256), 0)
    fence = jnp.where((lane == WIDTH) & (row >= SEQ), -1e30, 0.0).astype(BF)
    flag = jnp.where(lane == WIDTH, 1.0, 0.0).astype(BF)
    zero = jnp.zeros((PAD, 256 - WIDTH), BF)
    total = None
    for r in range(2):
        qk = dot_nn(x, h1_ref[:, r * 2 * WIDTH : (r + 1) * 2 * WIDTH])
        q = ((qk[:, :WIDTH] + qb_ref[r]) * (1.0 / math.sqrt(HD))).astype(BF)
        k = qk[:, WIDTH:].astype(BF)
        v = (dot_nn(x, h2_ref[:, r * 2 * WIDTH : r * 2 * WIDTH + WIDTH]) + vb_ref[r]).astype(BF)
        q_ref[r] = q
        k_ref[r] = k
        v_ref[r] = v
        q_wide = jnp.concatenate([q, zero], axis=1)
        k_wide = jnp.concatenate([k, zero], axis=1) + fence
        v_t = v.astype(F32).T.astype(BF)
        att_t = []
        for h in range(HEADS):
            mine = (lane >= h * HD) & (lane < (h + 1) * HD)
            s = dot_nt(k_wide, jnp.where(mine, q_wide, flag))
            e = jnp.exp(s - jnp.max(s, axis=0, keepdims=True))
            p = (e * (1.0 / jnp.sum(e, axis=0, keepdims=True))).astype(BF)
            p_ref[r * HEADS + h] = p
            att_t.append(dot_nn(v_t[h * HD : (h + 1) * HD], p))
        att = jnp.concatenate(att_t, axis=0).T.astype(BF)
        att_ref[r] = att
        mixed = dot_nt(att, h2_ref[:, r * 2 * WIDTH + WIDTH : (r + 1) * 2 * WIDTH])
        total = mixed if r == 0 else total + mixed
    out_ref[...] = total.astype(BF)


def attend(normed, h1, h2, qb, vb):
    rows, dim = normed.shape
    images = rows // PAD
    act = pl.BlockSpec((2, PAD, WIDTH), lambda i: (0, i, 0))
    act_shape = jax.ShapeDtypeStruct((2, rows, WIDTH), BF)
    return pl.pallas_call(
        attend_kernel,
        grid=(images,),
        in_specs=[
            row_block(dim),
            whole(dim, 4 * WIDTH),
            whole(dim, 4 * WIDTH),
            whole(2, 1, WIDTH),
            whole(2, 1, WIDTH),
        ],
        out_specs=[
            act,
            act,
            act,
            act,
            pl.BlockSpec((2 * HEADS, PAD, PAD), lambda i: (i, 0, 0)),
            row_block(dim),
        ],
        out_shape=[
            act_shape,
            act_shape,
            act_shape,
            act_shape,
            jax.ShapeDtypeStruct((2 * HEADS * images, PAD, PAD), BF),
            jax.ShapeDtypeStruct((rows, dim), BF),
        ],
        name="attend",
    )(normed, h1, h2, qb, vb)


def attend_back_kernel(
    g_ref, q_ref, k_ref, v_ref, p_ref, h1_ref, h2_ref, dq_ref, dk_ref, dv_ref, out_ref, qs_ref, vs_ref
):
    g = g_ref[...]
    scale = 1.0 / math.sqrt(HD)
    lane = lax.broadcasted_iota(jnp.int32, (PAD, WIDTH), 1)
    total = None

    @pl.when(pl.program_id(0) == 0)
    def _():
        qs_ref[...] = jnp.zeros_like(qs_ref)
        vs_ref[...] = jnp.zeros_like(vs_ref)

    for r in range(2):
        base = r * 2 * WIDTH
        d_att = dot_nn(g, h2_ref[:, base + WIDTH : base + 2 * WIDTH]).astype(BF)
        q, k, v = q_ref[r], k_ref[r], v_ref[r]
        k_t = k.astype(F32).T.astype(BF)
        dq_t = []
        dk = jnp.zeros((PAD, WIDTH), F32)
        dv = jnp.zeros((PAD, WIDTH), F32)
        for h in range(HEADS):
            mine = (lane >= h * HD) & (lane < (h + 1) * HD)
            p = p_ref[r * HEADS + h]
            p32 = p.astype(F32)
            dp = dot_nt(jnp.where(mine, v, jnp.zeros_like(v)), d_att)
            delta = jnp.sum(p32 * dp, axis=0, keepdims=True)
            ds = (p32 * (dp - delta)).astype(BF)
            dv = jnp.where(mine, dot_nn(p, d_att), dv)
            dk = jnp.where(mine, dot_nn(ds, q), dk)
            dq_t.append(dot_nn(k_t[h * HD : (h + 1) * HD], ds))
        dq = jnp.concatenate(dq_t, axis=0).T * scale
        qs_ref[r] += jnp.sum(dq, axis=0, keepdims=True)
        vs_ref[r] += jnp.sum(dv, axis=0, keepdims=True)
        dq, dk, dv = dq.astype(BF), dk.astype(BF), dv.astype(BF)
        dq_ref[r] = dq
        dk_ref[r] = dk
        dv_ref[:, r * WIDTH : (r + 1) * WIDTH] = dv
        piece = dot_nt(dq, h1_ref[:, base : base + WIDTH])
        piece = piece + dot_nt(dk, h1_ref[:, base + WIDTH : base + 2 * WIDTH])
        piece = piece + dot_nt(dv, h2_ref[:, base : base + WIDTH])
        total = piece if r == 0 else total + piece
    out_ref[...] = total.astype(BF)


def attend_back(grad, q, k, v, p, h1, h2):
    rows, dim = grad.shape
    images = rows // PAD
    act = pl.BlockSpec((2, PAD, WIDTH), lambda i: (0, i, 0))
    act_shape = jax.ShapeDtypeStruct((2, rows, WIDTH), BF)
    return pl.pallas_call(
        attend_back_kernel,
        grid=(images,),
        in_specs=[
            row_block(dim),
            act,
            act,
            act,
            pl.BlockSpec((2 * HEADS, PAD, PAD), lambda i: (i, 0, 0)),
            whole(dim, 4 * WIDTH),
            whole(dim, 4 * WIDTH),
        ],
        out_specs=[act, act, row_block(2 * WIDTH), row_block(dim), whole(2, 1, WIDTH), whole(2, 1, WIDTH)],
        out_shape=[
            act_shape,
            act_shape,
            jax.ShapeDtypeStruct((rows, 2 * WIDTH), BF),
            jax.ShapeDtypeStruct((rows, dim), BF),
            jax.ShapeDtypeStruct((2, 1, WIDTH), F32),
            jax.ShapeDtypeStruct((2, 1, WIDTH), F32),
        ],
        name="attend_back",
    )(grad, q, k, v, p, h1, h2)


def middle_kernel(v_ref, a_ref, b_ref, bias_ref, gain_ref, shift_ref, res_ref, norm_ref):
    mixed = a_ref[...].astype(F32) + b_ref[...].astype(F32)
    residual = v_ref[...].astype(F32) + mixed + bias_ref[...]
    centered, _ = center(residual)
    res_ref[...] = residual
    norm_ref[...] = (centered * gain_ref[...] + shift_ref[...]).astype(BF)


def middle(values, own, other, bias, gain, shift):
    rows, dim = values.shape
    return pl.pallas_call(
        middle_kernel,
        grid=(rows // PAD,),
        in_specs=[row_block(dim)] * 3 + [whole(1, dim)] * 3,
        out_specs=[row_block(dim)] * 2,
        out_shape=[jax.ShapeDtypeStruct((rows, dim), F32), jax.ShapeDtypeStruct((rows, dim), BF)],
        name="middle",
    )(values, own, other, bias, gain, shift)


def back_through(values, d_norm, gain):
    centered, inv_std = center(values)
    scaled = d_norm * gain
    crossed = d_norm * centered
    first = jnp.mean(scaled, axis=1, keepdims=True)
    second = jnp.mean(crossed * gain, axis=1, keepdims=True)
    d_values = inv_std * (scaled - first - centered * second)
    return d_values, jnp.sum(crossed, axis=0, keepdims=True), jnp.sum(d_norm, axis=0, keepdims=True)


def middle_back_kernel(res_ref, g_ref, a_ref, b_ref, gain_ref, dr_ref, drb_ref, sums_ref):
    d_norm = a_ref[...].astype(F32) + b_ref[...].astype(F32)
    d_ln, d_gain, d_shift = back_through(res_ref[...], d_norm, gain_ref[...])
    grad = g_ref[...].astype(F32)
    d_res = grad + d_ln
    dr_ref[...] = d_res
    drb_ref[...] = d_res.astype(BF)
    parts = [d_gain, d_shift, jnp.sum(d_res, axis=0, keepdims=True), jnp.sum(grad, axis=0, keepdims=True)]
    block = jnp.concatenate(parts + [jnp.zeros((4, d_gain.shape[1]), F32)], axis=0)

    @pl.when(pl.program_id(0) == 0)
    def _():
        sums_ref[...] = block

    @pl.when(pl.program_id(0) != 0)
    def _():
        sums_ref[...] += block


def middle_back(residual, grads, own, other, gain):
    rows, dim = residual.shape
    return pl.pallas_call(
        middle_back_kernel,
        grid=(rows // PAD,),
        in_specs=[row_block(dim)] * 4 + [whole(1, dim)],
        out_specs=[row_block(dim), row_block(dim), whole(8, dim)],
        out_shape=[
            jax.ShapeDtypeStruct((rows, dim), F32),
            jax.ShapeDtypeStruct((rows, dim), BF),
            jax.ShapeDtypeStruct((8, dim), F32),
        ],
        name="middle_back",
    )(residual, grads, own, other, gain)


def pack_rows(values, order_ref, select_ref, own_ref, far_ref):
    cols = dot_nn(values.astype(BF), order_ref[...]).astype(BF)
    for t in range(2):
        rows = dot_nn(select_ref[t], cols).astype(BF)
        own_ref[:, t * WIDTH : (t + 1) * WIDTH] = rows[:, :WIDTH]
        far_ref[:, t * WIDTH : (t + 1) * WIDTH] = rows[:, WIDTH:]


def output_kernel(res_ref, a_ref, b_ref, bias_ref, order_ref, select_ref, own_ref, far_ref):
    values = res_ref[...] + (a_ref[...].astype(F32) + b_ref[...].astype(F32)) + bias_ref[...]
    pack_rows(values, order_ref, select_ref, own_ref, far_ref)


def input_kernel(dr_ref, a_ref, b_ref, v_ref, gain_ref, order_ref, select_ref, own_ref, far_ref, sums_ref):
    d_norm = a_ref[...].astype(F32) + b_ref[...].astype(F32)
    d_ln, d_gain, d_shift = back_through(v_ref[...].astype(F32), d_norm, gain_ref[...])
    sums_ref[...] = jnp.concatenate([d_gain, d_shift, jnp.zeros((6, d_gain.shape[1]), F32)], axis=0)
    pack_rows(dr_ref[...] + d_ln, order_ref, select_ref, own_ref, far_ref)


def pack(kernel, operands, order, select, sums):
    part = select.shape[1]
    dim = order.shape[0]
    ref = pl.BlockSpec(memory_space=pltpu.VMEM)
    shapes = [jax.ShapeDtypeStruct((part, 2 * WIDTH), BF)] * 2
    if sums:
        shapes = shapes + [jax.ShapeDtypeStruct((8, dim), F32)]
    return pl.pallas_call(
        kernel,
        in_specs=[ref] * (len(operands) + 2),
        out_specs=[ref] * len(shapes),
        out_shape=shapes,
        name="pack_input" if sums else "pack_output",
    )(*operands, order, select)


def body(
    block_input,
    norm_gain1,
    norm_shift1,
    qkv_weight,
    query_bias,
    value_bias,
    out_weight,
    out_bias,
    norm_gain2,
    norm_shift2,
    up_weight,
    up_bias,
    down_weight,
    down_bias,
    out_grad,
):
    feat = lax.axis_index("feat")
    tok = lax.axis_index("tok")
    x, core = feat // 2, feat % 2
    rows = block_input.shape[0]
    local = block_input.shape[1] // 2
    dim = local * lax.axis_size("feat")
    bits = tok_bits()
    block = dim >> bits
    part = (rows + 1) // 2
    shift_rows = rows - part
    images = rows // SEQ
    first_token = x * rows - 2 * x * shift_rows

    def selection(slot, source):
        seat = slot % PAD
        token = first_token + (slot // PAD) * SEQ + seat
        return (seat < SEQ) & (source == token)

    shape = (2, images * PAD, EDGE)
    hit = selection(
        lax.broadcasted_iota(jnp.int32, shape, 1),
        2 * lax.broadcasted_iota(jnp.int32, shape, 2) + lax.broadcasted_iota(jnp.int32, shape, 0),
    )
    select = jnp.where(hit, 1.0, 0.0).astype(BF)
    shape = (2, part, images * PAD)
    hit = selection(
        lax.broadcasted_iota(jnp.int32, shape, 2),
        2 * lax.broadcasted_iota(jnp.int32, shape, 1) + lax.broadcasted_iota(jnp.int32, shape, 0),
    )
    select_back = jnp.where(hit, 1.0, 0.0).astype(BF)

    def feature_of_piece(col):
        piece = col // local
        owner = 2 * (x ^ (piece % 2)) + (core ^ (piece // 2))
        return owner * local + col % local

    def feature_of_row(col):
        j = col // block
        mask = sum(((j >> (bits - 1 - k)) & 1) << k for k in range(bits))
        return (tok ^ mask) * block + col % block

    line = jnp.arange(dim, dtype=jnp.int32)
    by_piece, by_row = feature_of_piece(line), feature_of_row(line)
    order = jnp.where(by_piece[:, None] == by_row[None, :], 1.0, 0.0).astype(BF)
    order_back = jnp.where(by_row[:, None] == by_piece[None, : dim // 2], 1.0, 0.0).astype(BF)

    a_pair = jnp.stack(
        [
            qkv_weight[:, :2, :].reshape(-1, 2 * local),
            jnp.concatenate([qkv_weight[:, 2, :], out_weight.T], axis=1),
        ]
    )
    a_seen = a_pair
    own_small = jnp.concatenate(
        [norm_gain1, norm_shift1, norm_gain2, norm_shift2, out_bias, down_bias]
        + [query_bias, value_bias, up_bias]
    ).reshape(-1, 128)
    own_in = lax.dynamic_slice_in_dim(block_input, x * shift_rows, part, 0)
    sent_in = lax.dynamic_slice_in_dim(block_input, (1 - x) * shift_rows, part, 0)
    own_out = lax.dynamic_slice_in_dim(out_grad, x * shift_rows, part, 0)
    sent_out = lax.dynamic_slice_in_dim(out_grad, (1 - x) * shift_rows, part, 0)

    marks = []
    for k in outer_bits():
        got = swap(a_seen, "tok", 1 << k)
        marks.append(got)
        a_seen = jnp.concatenate([a_seen, got], axis=1)
    far_small = swap_x(own_small)
    pair_in = jnp.stack([own_in, swap_x(sent_in)])
    other_in = swap_core(pair_in)
    pair_out = jnp.stack([own_out, swap_x(sent_out)])
    other_out = swap_core(pair_out)

    b_own, c_own = up_weight, down_weight.T
    b_far = swap_x(after(b_own, pair_out))
    c_side = swap_y(c_own)
    b_pair = jnp.stack([b_own, b_far])
    c_pair = jnp.stack([c_own, c_side])
    b_pair_side = swap_y(b_pair)
    c_pair_far = swap_x(c_pair)

    def gather_z(own, gate):
        seen, parts = own, []
        for i, k in enumerate(outer_bits()):
            got = swap(after(seen, gate) if i == 0 else seen, "tok", 1 << k)
            parts.append(got)
            seen = jnp.concatenate([seen, got], axis=0)
        return jnp.concatenate(parts, axis=0)

    b_rest = gather_z(b_own, marks[0])
    c_rest = gather_z(c_own, marks[-1])

    h1_y = swap_y(a_seen[0])
    h2_x = swap_x(a_seen[1])
    h1_near = jnp.concatenate([a_seen[0], h1_y], axis=0)
    h2_near = jnp.stack([a_seen[1], h2_x])
    h1_far = swap_x(h1_near)
    h2_y = swap_y(h2_near)
    h1 = jnp.concatenate([h1_near, h1_far], axis=1)
    h2 = jnp.concatenate([h2_near, h2_y], axis=1)
    h2 = jnp.concatenate([h2[0], h2[1]], axis=1)

    b_rest_far = swap_x(after(b_rest, h2_x))
    c_rest_side = swap_y(after(c_rest, h1_y))
    b_rest_pair = jnp.stack([b_rest, b_rest_far])
    c_rest_pair = jnp.stack([c_rest, c_rest_side])
    b_rest_pair_side = swap_y(after(b_rest_pair, h2_y))
    c_rest_pair_far = swap_x(after(c_rest_pair, h1_far))
    up = jnp.concatenate(
        [
            jnp.concatenate([b_pair[i], b_rest_pair[i], b_pair_side[i], b_rest_pair_side[i]], axis=0)
            for i in range(2)
        ],
        axis=1,
    )
    down = jnp.concatenate(
        [
            jnp.concatenate([c_pair[0], c_rest_pair[0], c_pair[1], c_rest_pair[1]], axis=0),
            jnp.concatenate(
                [c_pair_far[0], c_rest_pair_far[0], c_pair_far[1], c_rest_pair_far[1]], axis=0
            ),
        ],
        axis=1,
    )

    pair_small = jnp.stack([own_small.reshape(-1), far_small.reshape(-1)])
    qb = pair_small[:, 6 * local : 7 * local].reshape(2, 1, local)
    vb = pair_small[:, 7 * local : 8 * local].reshape(2, 1, local)
    upb = pair_small[:, 8 * local :].reshape(1, -1)
    wide = pair_small[:, : 6 * local].reshape(2, -1, 128)
    pieces = jnp.concatenate([wide, swap_core(wide)], axis=0).reshape(4, 6, local)
    pieces = pieces.transpose(1, 0, 2).reshape(6, dim)
    vectors = jnp.dot(pieces, order.astype(F32), precision=lax.Precision.HIGHEST)
    gain1, shift1, gain2, shift2, obias, dbias = [vectors[i : i + 1] for i in range(6)]

    values, normed1 = tokens(pair_in, other_in, select, order, gain1, shift1)
    (grads,) = tokens(pair_out, other_out, select, order)
    q, k, v, att, probs, mixed = attend(normed1, h1, h2, qb, vb)
    residual, normed2 = middle(values, mixed, swap_core(mixed), obias, gain2, shift2)

    before = dot_nn(normed2, up) + upb
    cdf = 0.5 * (1.0 + lax.erf(before * HALF_ROOT))
    hidden = (before * cdf).astype(BF)
    slope = cdf + before * jnp.exp(-0.5 * before * before) * INV_ROOT_TWO_PI
    d_before = dot_nn(grads, down) * slope
    d_before_b = d_before.astype(BF)
    dn2 = dot_nt(d_before_b, up).astype(BF)
    dn2_other = swap_core(dn2)
    wide_cols = up.shape[1] // 2
    half = dim // 2
    gc_far = dot_tn(grads, hidden[:, wide_cols:]).astype(BF)
    gc_own = dot_tn(grads, hidden[:, :wide_cols]).astype(BF)
    gb_far = dot_tn(normed2[:, half:], d_before_b).astype(BF)
    gb_own = dot_tn(normed2[:, :half], d_before_b).astype(BF)
    down_out = dot_nt(hidden, down).astype(BF)
    down_other = swap_core(down_out)

    def scatter_x_first(own, far):
        total = add_rows(own, swap_x(far))
        kept, sent = total[:half], total[half:].astype(BF)
        return scatter_outer(add_rows(kept, swap_y(sent)))

    def scatter_y_first(own, far, split):
        total = add_rows(own, swap_y(far))
        kept, sent = split(total)
        return scatter_outer(add_rows(kept, swap_x(sent.astype(BF))))

    grad_down = scatter_x_first(gc_own, gc_far)
    grad_up = scatter_y_first(gb_own, gb_far, lambda t: (t[:, :wide_cols], t[:, wide_cols:]))

    def put_together(own, far):
        got = swap_x(far)
        low = jnp.where(x == 0, own, got).astype(F32)
        high = jnp.where(x == 0, got, own).astype(F32)
        return jnp.pad(low, ((0, shift_rows), (0, 0))) + jnp.pad(high, ((shift_rows, 0), (0, 0)))

    out_own, out_far = pack(
        output_kernel, (residual, down_out, down_other, dbias), order_back, select_back, False
    )
    block_output = put_together(out_own, out_far).astype(BF)

    d_resid, d_resid_b, sums2 = middle_back(residual, grads, dn2, dn2_other, gain2)
    dq, dk, dv, dn1, q_sum, v_sum = attend_back(d_resid_b, q, k, v, probs, h1, h2)
    dn1_other = swap_core(dn1)
    qk_own = jnp.concatenate([dot_tn(normed1, dq[0]), dot_tn(normed1, dk[0])], axis=1).astype(BF)
    qk_far = jnp.concatenate([dot_tn(normed1, dq[1]), dot_tn(normed1, dk[1])], axis=1).astype(BF)
    att_all = jnp.concatenate([att[0], att[1]], axis=1)

    def value_grads(cols):
        return jnp.concatenate(
            [dot_tn(normed1[:, cols], dv), dot_tn(d_resid_b[:, cols], att_all)], axis=1
        ).astype(BF)

    vo_far = value_grads(slice(half, dim))
    vo_own = value_grads(slice(0, half))
    grad_qk = scatter_x_first(qk_own, qk_far)

    def split_vo(total):
        cut = [total[:, i * local : (i + 1) * local] for i in range(4)]
        return jnp.concatenate([cut[0], cut[2]], axis=1), jnp.concatenate([cut[1], cut[3]], axis=1)

    grad_vo = scatter_y_first(vo_own, vo_far, split_vo)
    in_own, in_far, sums1 = pack(
        input_kernel, (d_resid, dn1, dn1_other, values, gain1), order_back, select_back, True
    )
    input_grad = put_together(in_own, in_far)

    vecs = jnp.concatenate([sums1[:2], sums2[:4]], axis=0)
    vecs = jnp.dot(vecs, order_back.astype(F32), precision=lax.Precision.HIGHEST)
    up_sum = jnp.sum(d_before, axis=0)
    small = [
        jnp.concatenate(
            [vecs[:, i * local : (i + 1) * local].reshape(-1), q_sum[i, 0], v_sum[i, 0]]
            + [up_sum[i * wide_cols : (i + 1) * wide_cols]]
        ).reshape(-1, 128)
        for i in range(2)
    ]
    total = small[0] + swap_x(small[1])
    for i in range(bits):
        total = total + swap(total, "tok", 1 << i)
    total = total.reshape(-1)
    cut = lambda i: total[i * local : (i + 1) * local]

    return (
        block_output,
        input_grad,
        cut(0),
        cut(1),
        jnp.concatenate([grad_qk, grad_vo[:, :local]], axis=1).reshape(qkv_weight.shape),
        cut(6),
        cut(7),
        grad_vo[:, local:].T,
        cut(4),
        cut(2),
        cut(3),
        grad_up,
        total[8 * local :],
        grad_down.T,
        cut(5),
    )


def solution(mesh):
    vec = P("feat")
    act = P("tok", "feat")
    qkv = P("tok", None, "feat")
    turned = P("feat", "tok")
    in_specs = (act, vec, vec, qkv, vec, vec, turned, vec, vec, vec, act, vec, turned, vec, act)
    out_specs = (act, act, vec, vec, qkv, vec, vec, turned, vec, vec, vec, act, vec, turned, vec)
    return jax.shard_map(body, mesh=mesh, in_specs=in_specs, out_specs=out_specs, check_vma=False)
```

```python
import math

import jax
import jax.numpy as jnp
from jax import lax
from jax.experimental import pallas as pl
from jax.experimental.pallas import tpu as pltpu
from jax.sharding import PartitionSpec as P

HD = 64
SEQ = 197
PAD = 208
HEADS = 3
WIDTH = HEADS * HD
EDGE = 384
COLS = 512
HALF_ROOT = 0.7071067811865476
INV_ROOT_TWO_PI = 0.3989422804014327
EPSILON = 1e-06
BF = jnp.bfloat16
F32 = jnp.float32


def dot_nn(left, right):
    return lax.dot_general(left, right, (((1,), (0,)), ((), ())), preferred_element_type=F32)


def dot_nt(left, right):
    return lax.dot_general(left, right, (((1,), (1,)), ((), ())), preferred_element_type=F32)


def dot_tn(left, right):
    return lax.dot_general(left, right, (((0,), (0,)), ((), ())), preferred_element_type=F32)


def swap(values, axis, bit):
    size = lax.axis_size(axis)
    return lax.ppermute(values, axis, [(i, i ^ bit) for i in range(size)])


def swap_x(values):
    return swap(values, "feat", 2)


def swap_core(values):
    return swap(values, "feat", 1)


def swap_y(values):
    return swap(values, "tok", 1)


def after(value, *others):
    return lax.optimization_barrier((value,) + others)[0]


def tok_bits():
    return int(math.log2(lax.axis_size("tok")))


def outer_bits():
    return range(tok_bits() - 1, 0, -1)


def add_rows(kept, got):
    return kept.astype(F32) + got.astype(F32)


def scatter_outer(total):
    for k in reversed(outer_bits()):
        half = total.shape[0] // 2
        kept, sent = total[:half], total[half:]
        total = add_rows(kept, swap(sent.astype(BF), "tok", 1 << k))
    return total


def whole(*shape):
    return pl.BlockSpec(shape, lambda i: (0,) * len(shape))


def row_block(width):
    return pl.BlockSpec((PAD, width), lambda i: (i, 0))


def place(own_ref, far_ref, scratch):
    part = own_ref.shape[1]
    scratch[...] = jnp.zeros_like(scratch)
    for piece in range(4):
        rows = (own_ref if piece < 2 else far_ref)[piece % 2]
        for t in range(2):
            scratch[t, 0:part, piece * WIDTH : (piece + 1) * WIDTH] = rows[:, t * WIDTH : (t + 1) * WIDTH]


def tokens_kernel(own_ref, far_ref, select_ref, order_ref, out_ref, scratch):
    @pl.when(pl.program_id(0) == 0)
    def _():
        place(own_ref, far_ref, scratch)

    rows = dot_nn(select_ref[0], scratch[0]) + dot_nn(select_ref[1], scratch[1])
    out_ref[...] = dot_nn(rows.astype(BF), order_ref[...]).astype(BF)


def tokens_norm_kernel(own_ref, far_ref, select_ref, order_ref, gain_ref, shift_ref, out_ref, norm_ref, scratch):
    @pl.when(pl.program_id(0) == 0)
    def _():
        place(own_ref, far_ref, scratch)

    rows = dot_nn(select_ref[0], scratch[0]) + dot_nn(select_ref[1], scratch[1])
    values = dot_nn(rows.astype(BF), order_ref[...])
    out_ref[...] = values.astype(BF)
    centered, _ = center(values)
    norm_ref[...] = (centered * gain_ref[...] + shift_ref[...]).astype(BF)


def tokens(own, far, select, order, gain=None, shift=None):
    part, dim = own.shape[1], order.shape[0]
    rows = select.shape[1]
    normed = gain is not None
    vec = [gain, shift] if normed else []
    count = 2 if normed else 1
    return pl.pallas_call(
        tokens_norm_kernel if normed else tokens_kernel,
        grid=(rows // PAD,),
        in_specs=[
            whole(2, part, 2 * WIDTH),
            whole(2, part, 2 * WIDTH),
            pl.BlockSpec((2, PAD, EDGE), lambda i: (0, i, 0)),
            whole(dim, dim),
        ]
        + [whole(1, dim)] * len(vec),
        out_specs=[row_block(dim)] * count,
        out_shape=[jax.ShapeDtypeStruct((rows, dim), BF)] * count,
        scratch_shapes=[pltpu.VMEM((2, EDGE, dim), BF)],
        name="tokens_norm" if normed else "tokens",
        compiler_params=pltpu.CompilerParams(vmem_limit_bytes=20 << 20),
    )(own, far, select, order, *vec)


def center(values):
    mean_val = jnp.mean(values, axis=1, keepdims=True)
    variance = jnp.mean(values * values, axis=1, keepdims=True) - mean_val * mean_val
    inv_std = lax.rsqrt(variance + EPSILON)
    return (values - mean_val) * inv_std, inv_std


def attend_kernel(x_ref, h1_ref, h2_ref, qb_ref, vb_ref, q_ref, k_ref, v_ref, att_ref, p_ref, out_ref):
    x = x_ref[...]
    lane = lax.broadcasted_iota(jnp.int32, (PAD, 256), 1)
    row = lax.broadcasted_iota(jnp.int32, (PAD, 256), 0)
    fence = jnp.where((lane == WIDTH) & (row >= SEQ), -1e30, 0.0).astype(BF)
    flag = jnp.where(lane == WIDTH, 1.0, 0.0).astype(BF)
    zero = jnp.zeros((PAD, 256 - WIDTH), BF)
    total = None
    for r in range(2):
        qk = dot_nn(x, h1_ref[:, r * 2 * WIDTH : (r + 1) * 2 * WIDTH])
        q = ((qk[:, :WIDTH] + qb_ref[r]) * (1.0 / math.sqrt(HD))).astype(BF)
        k = qk[:, WIDTH:].astype(BF)
        v = (dot_nn(x, h2_ref[:, r * 2 * WIDTH : r * 2 * WIDTH + WIDTH]) + vb_ref[r]).astype(BF)
        q_ref[r] = q
        k_ref[r] = k
        v_ref[r] = v
        q_wide = jnp.concatenate([q, zero], axis=1)
        k_wide = jnp.concatenate([k, zero], axis=1) + fence
        v_t = v.astype(F32).T.astype(BF)
        att_t = []
        for h in range(HEADS):
            mine = (lane >= h * HD) & (lane < (h + 1) * HD)
            s = dot_nt(k_wide, jnp.where(mine, q_wide, flag))
            e = jnp.exp(s - jnp.max(s, axis=0, keepdims=True))
            p = (e * (1.0 / jnp.sum(e, axis=0, keepdims=True))).astype(BF)
            p_ref[r * HEADS + h] = p
            att_t.append(dot_nn(v_t[h * HD : (h + 1) * HD], p))
        att = jnp.concatenate(att_t, axis=0).T.astype(BF)
        att_ref[r] = att
        mixed = dot_nt(att, h2_ref[:, r * 2 * WIDTH + WIDTH : (r + 1) * 2 * WIDTH])
        total = mixed if r == 0 else total + mixed
    out_ref[...] = total.astype(BF)


def attend(normed, h1, h2, qb, vb):
    rows, dim = normed.shape
    images = rows // PAD
    act = pl.BlockSpec((2, PAD, WIDTH), lambda i: (0, i, 0))
    act_shape = jax.ShapeDtypeStruct((2, rows, WIDTH), BF)
    return pl.pallas_call(
        attend_kernel,
        grid=(images,),
        in_specs=[
            row_block(dim),
            whole(dim, 4 * WIDTH),
            whole(dim, 4 * WIDTH),
            whole(2, 1, WIDTH),
            whole(2, 1, WIDTH),
        ],
        out_specs=[
            act,
            act,
            act,
            act,
            pl.BlockSpec((2 * HEADS, PAD, PAD), lambda i: (i, 0, 0)),
            row_block(dim),
        ],
        out_shape=[
            act_shape,
            act_shape,
            act_shape,
            act_shape,
            jax.ShapeDtypeStruct((2 * HEADS * images, PAD, PAD), BF),
            jax.ShapeDtypeStruct((rows, dim), BF),
        ],
        name="attend",
        compiler_params=pltpu.CompilerParams(vmem_limit_bytes=20 << 20),
    )(normed, h1, h2, qb, vb)


def attend_back_kernel(
    g_ref, q_ref, k_ref, v_ref, p_ref, h1_ref, h2_ref, dq_ref, dk_ref, dv_ref, out_ref, qs_ref, vs_ref
):
    g = g_ref[...]
    scale = 1.0 / math.sqrt(HD)
    lane = lax.broadcasted_iota(jnp.int32, (PAD, WIDTH), 1)
    total = None

    @pl.when(pl.program_id(0) == 0)
    def _():
        qs_ref[...] = jnp.zeros_like(qs_ref)
        vs_ref[...] = jnp.zeros_like(vs_ref)

    for r in range(2):
        base = r * 2 * WIDTH
        d_att = dot_nn(g, h2_ref[:, base + WIDTH : base + 2 * WIDTH]).astype(BF)
        q, k, v = q_ref[r], k_ref[r], v_ref[r]
        k_t = k.astype(F32).T.astype(BF)
        dq_t = []
        dk = jnp.zeros((PAD, WIDTH), F32)
        dv = jnp.zeros((PAD, WIDTH), F32)
        for h in range(HEADS):
            mine = (lane >= h * HD) & (lane < (h + 1) * HD)
            p = p_ref[r * HEADS + h]
            p32 = p.astype(F32)
            dp = dot_nt(jnp.where(mine, v, jnp.zeros_like(v)), d_att)
            delta = jnp.sum(p32 * dp, axis=0, keepdims=True)
            ds = (p32 * (dp - delta)).astype(BF)
            dv = jnp.where(mine, dot_nn(p, d_att), dv)
            dk = jnp.where(mine, dot_nn(ds, q), dk)
            dq_t.append(dot_nn(k_t[h * HD : (h + 1) * HD], ds))
        dq = jnp.concatenate(dq_t, axis=0).T * scale
        qs_ref[r] += jnp.sum(dq, axis=0, keepdims=True)
        vs_ref[r] += jnp.sum(dv, axis=0, keepdims=True)
        dq, dk, dv = dq.astype(BF), dk.astype(BF), dv.astype(BF)
        dq_ref[r] = dq
        dk_ref[r] = dk
        dv_ref[:, r * WIDTH : (r + 1) * WIDTH] = dv
        piece = dot_nt(dq, h1_ref[:, base : base + WIDTH])
        piece = piece + dot_nt(dk, h1_ref[:, base + WIDTH : base + 2 * WIDTH])
        piece = piece + dot_nt(dv, h2_ref[:, base : base + WIDTH])
        total = piece if r == 0 else total + piece
    out_ref[...] = total.astype(BF)


def attend_back(grad, q, k, v, p, h1, h2):
    rows, dim = grad.shape
    images = rows // PAD
    act = pl.BlockSpec((2, PAD, WIDTH), lambda i: (0, i, 0))
    act_shape = jax.ShapeDtypeStruct((2, rows, WIDTH), BF)
    return pl.pallas_call(
        attend_back_kernel,
        grid=(images,),
        in_specs=[
            row_block(dim),
            act,
            act,
            act,
            pl.BlockSpec((2 * HEADS, PAD, PAD), lambda i: (i, 0, 0)),
            whole(dim, 4 * WIDTH),
            whole(dim, 4 * WIDTH),
        ],
        out_specs=[act, act, row_block(2 * WIDTH), row_block(dim), whole(2, 1, WIDTH), whole(2, 1, WIDTH)],
        out_shape=[
            act_shape,
            act_shape,
            jax.ShapeDtypeStruct((rows, 2 * WIDTH), BF),
            jax.ShapeDtypeStruct((rows, dim), BF),
            jax.ShapeDtypeStruct((2, 1, WIDTH), F32),
            jax.ShapeDtypeStruct((2, 1, WIDTH), F32),
        ],
        name="attend_back",
        compiler_params=pltpu.CompilerParams(vmem_limit_bytes=20 << 20),
    )(grad, q, k, v, p, h1, h2)


def middle_kernel(v_ref, a_ref, b_ref, bias_ref, gain_ref, shift_ref, res_ref, norm_ref):
    mixed = a_ref[...].astype(F32) + b_ref[...].astype(F32)
    residual = v_ref[...].astype(F32) + mixed + bias_ref[...]
    centered, _ = center(residual)
    res_ref[...] = residual
    norm_ref[...] = (centered * gain_ref[...] + shift_ref[...]).astype(BF)


def middle(values, own, other, bias, gain, shift):
    rows, dim = values.shape
    return pl.pallas_call(
        middle_kernel,
        grid=(rows // PAD,),
        in_specs=[row_block(dim)] * 3 + [whole(1, dim)] * 3,
        out_specs=[row_block(dim)] * 2,
        out_shape=[jax.ShapeDtypeStruct((rows, dim), F32), jax.ShapeDtypeStruct((rows, dim), BF)],
        name="middle",
        compiler_params=pltpu.CompilerParams(vmem_limit_bytes=20 << 20),
    )(values, own, other, bias, gain, shift)


def back_through(values, d_norm, gain):
    centered, inv_std = center(values)
    scaled = d_norm * gain
    crossed = d_norm * centered
    first = jnp.mean(scaled, axis=1, keepdims=True)
    second = jnp.mean(crossed * gain, axis=1, keepdims=True)
    d_values = inv_std * (scaled - first - centered * second)
    return d_values, jnp.sum(crossed, axis=0, keepdims=True), jnp.sum(d_norm, axis=0, keepdims=True)


def middle_back_kernel(res_ref, g_ref, a_ref, b_ref, gain_ref, dr_ref, drb_ref, sums_ref):
    d_norm = a_ref[...].astype(F32) + b_ref[...].astype(F32)
    d_ln, d_gain, d_shift = back_through(res_ref[...], d_norm, gain_ref[...])
    grad = g_ref[...].astype(F32)
    d_res = grad + d_ln
    dr_ref[...] = d_res
    drb_ref[...] = d_res.astype(BF)
    parts = [d_gain, d_shift, jnp.sum(d_res, axis=0, keepdims=True), jnp.sum(grad, axis=0, keepdims=True)]
    block = jnp.concatenate(parts + [jnp.zeros((4, d_gain.shape[1]), F32)], axis=0)

    @pl.when(pl.program_id(0) == 0)
    def _():
        sums_ref[...] = block

    @pl.when(pl.program_id(0) != 0)
    def _():
        sums_ref[...] += block


def middle_back(residual, grads, own, other, gain):
    rows, dim = residual.shape
    return pl.pallas_call(
        middle_back_kernel,
        grid=(rows // PAD,),
        in_specs=[row_block(dim)] * 4 + [whole(1, dim)],
        out_specs=[row_block(dim), row_block(dim), whole(8, dim)],
        out_shape=[
            jax.ShapeDtypeStruct((rows, dim), F32),
            jax.ShapeDtypeStruct((rows, dim), BF),
            jax.ShapeDtypeStruct((8, dim), F32),
        ],
        name="middle_back",
        compiler_params=pltpu.CompilerParams(vmem_limit_bytes=20 << 20),
    )(residual, grads, own, other, gain)


def hidden_kernel(norm_ref, up_ref, bias_ref, hidden_ref, slope_ref):
    def step(j, _):
        c = pl.ds(pl.multiple_of(j * COLS, COLS), COLS)
        for i in range(norm_ref.shape[0] // PAD):
            r = slice(i * PAD, (i + 1) * PAD)
            before = dot_nn(norm_ref[r, :], up_ref[:, c]) + bias_ref[:, c]
            cdf = 0.5 * (1.0 + lax.erf(before * HALF_ROOT))
            hidden_ref[r, c] = (before * cdf).astype(BF)
            slope_ref[r, c] = cdf + before * jnp.exp(-0.5 * before * before) * INV_ROOT_TWO_PI
        return 0

    lax.fori_loop(0, up_ref.shape[1] // COLS, step, 0)


def hidden_back_kernel(g_ref, down_ref, slope_ref, up_ref, db_ref, out_ref, sum_ref, acc_ref):
    acc_ref[...] = jnp.zeros_like(acc_ref)

    def step(j, _):
        c = pl.ds(pl.multiple_of(j * COLS, COLS), COLS)
        total = jnp.zeros((1, COLS), F32)
        for i in range(g_ref.shape[0] // PAD):
            r = slice(i * PAD, (i + 1) * PAD)
            d_before = dot_nn(g_ref[r, :], down_ref[:, c]) * slope_ref[r, c]
            total = total + jnp.sum(d_before, axis=0, keepdims=True)
            rounded = d_before.astype(BF)
            db_ref[r, c] = rounded
            acc_ref[r, :] += dot_nt(rounded, up_ref[:, c])
        sum_ref[:, c] = total
        return 0

    lax.fori_loop(0, up_ref.shape[1] // COLS, step, 0)
    out_ref[...] = acc_ref[...].astype(BF)


def resident(kernel, shapes, *operands, scratch=(), name):
    ref = pl.BlockSpec(memory_space=pltpu.VMEM)
    return pl.pallas_call(
        kernel,
        in_specs=[ref] * len(operands),
        out_specs=[ref] * len(shapes),
        out_shape=[jax.ShapeDtypeStruct(shape, dtype) for shape, dtype in shapes],
        scratch_shapes=list(scratch),
        name=name,
        compiler_params=pltpu.CompilerParams(vmem_limit_bytes=20 << 20),
    )(*operands)


def pack_rows(values, order_ref, select_ref, own_ref, far_ref):
    cols = dot_nn(values.astype(BF), order_ref[...]).astype(BF)
    for t in range(2):
        rows = dot_nn(select_ref[t], cols).astype(BF)
        own_ref[:, t * WIDTH : (t + 1) * WIDTH] = rows[:, :WIDTH]
        far_ref[:, t * WIDTH : (t + 1) * WIDTH] = rows[:, WIDTH:]


def output_kernel(res_ref, a_ref, b_ref, bias_ref, order_ref, select_ref, own_ref, far_ref):
    values = res_ref[...] + (a_ref[...].astype(F32) + b_ref[...].astype(F32)) + bias_ref[...]
    pack_rows(values, order_ref, select_ref, own_ref, far_ref)


def input_kernel(dr_ref, a_ref, b_ref, v_ref, gain_ref, order_ref, select_ref, own_ref, far_ref, sums_ref):
    d_norm = a_ref[...].astype(F32) + b_ref[...].astype(F32)
    d_ln, d_gain, d_shift = back_through(v_ref[...].astype(F32), d_norm, gain_ref[...])
    sums_ref[...] = jnp.concatenate([d_gain, d_shift, jnp.zeros((6, d_gain.shape[1]), F32)], axis=0)
    pack_rows(dr_ref[...] + d_ln, order_ref, select_ref, own_ref, far_ref)


def pack(kernel, operands, order, select, sums):
    part = select.shape[1]
    dim = order.shape[0]
    ref = pl.BlockSpec(memory_space=pltpu.VMEM)
    shapes = [jax.ShapeDtypeStruct((part, 2 * WIDTH), BF)] * 2
    if sums:
        shapes = shapes + [jax.ShapeDtypeStruct((8, dim), F32)]
    return pl.pallas_call(
        kernel,
        in_specs=[ref] * (len(operands) + 2),
        out_specs=[ref] * len(shapes),
        out_shape=shapes,
        name="pack_input" if sums else "pack_output",
        compiler_params=pltpu.CompilerParams(vmem_limit_bytes=20 << 20),
    )(*operands, order, select)


def body(
    block_input,
    norm_gain1,
    norm_shift1,
    qkv_weight,
    query_bias,
    value_bias,
    out_weight,
    out_bias,
    norm_gain2,
    norm_shift2,
    up_weight,
    up_bias,
    down_weight,
    down_bias,
    out_grad,
):
    feat = lax.axis_index("feat")
    tok = lax.axis_index("tok")
    x, core = feat // 2, feat % 2
    rows = block_input.shape[0]
    local = block_input.shape[1] // 2
    dim = local * lax.axis_size("feat")
    bits = tok_bits()
    block = dim >> bits
    part = (rows + 1) // 2
    shift_rows = rows - part
    images = rows // SEQ
    first_token = x * rows - 2 * x * shift_rows

    def selection(slot, source):
        seat = slot % PAD
        token = first_token + (slot // PAD) * SEQ + seat
        return (seat < SEQ) & (source == token)

    shape = (2, images * PAD, EDGE)
    hit = selection(
        lax.broadcasted_iota(jnp.int32, shape, 1),
        2 * lax.broadcasted_iota(jnp.int32, shape, 2) + lax.broadcasted_iota(jnp.int32, shape, 0),
    )
    select = jnp.where(hit, 1.0, 0.0).astype(BF)
    shape = (2, part, images * PAD)
    hit = selection(
        lax.broadcasted_iota(jnp.int32, shape, 2),
        2 * lax.broadcasted_iota(jnp.int32, shape, 1) + lax.broadcasted_iota(jnp.int32, shape, 0),
    )
    select_back = jnp.where(hit, 1.0, 0.0).astype(BF)

    def feature_of_piece(col):
        piece = col // local
        owner = 2 * (x ^ (piece % 2)) + (core ^ (piece // 2))
        return owner * local + col % local

    def feature_of_row(col):
        j = col // block
        mask = sum(((j >> (bits - 1 - k)) & 1) << k for k in range(bits))
        return (tok ^ mask) * block + col % block

    line = jnp.arange(dim, dtype=jnp.int32)
    by_piece, by_row = feature_of_piece(line), feature_of_row(line)
    order = jnp.where(by_piece[:, None] == by_row[None, :], 1.0, 0.0).astype(BF)
    order_back = jnp.where(by_row[:, None] == by_piece[None, : dim // 2], 1.0, 0.0).astype(BF)

    a_pair = jnp.stack(
        [
            qkv_weight[:, :2, :].reshape(-1, 2 * local),
            jnp.concatenate([qkv_weight[:, 2, :], out_weight.T], axis=1),
        ]
    )
    a_seen = a_pair
    own_small = jnp.concatenate(
        [norm_gain1, norm_shift1, norm_gain2, norm_shift2, out_bias, down_bias]
        + [query_bias, value_bias, up_bias]
    ).reshape(-1, 128)
    own_in = lax.dynamic_slice_in_dim(block_input, x * shift_rows, part, 0)
    sent_in = lax.dynamic_slice_in_dim(block_input, (1 - x) * shift_rows, part, 0)
    own_out = lax.dynamic_slice_in_dim(out_grad, x * shift_rows, part, 0)
    sent_out = lax.dynamic_slice_in_dim(out_grad, (1 - x) * shift_rows, part, 0)

    marks = []
    for k in outer_bits():
        got = swap(a_seen, "tok", 1 << k)
        marks.append(got)
        a_seen = jnp.concatenate([a_seen, got], axis=1)
    far_small = swap_x(own_small)
    pair_in = jnp.stack([own_in, swap_x(sent_in)])
    other_in = swap_core(pair_in)
    pair_out = jnp.stack([own_out, swap_x(sent_out)])
    other_out = swap_core(pair_out)

    b_own, c_own = up_weight, down_weight.T
    b_far = swap_x(after(b_own, pair_out))
    c_side = swap_y(c_own)
    b_pair = jnp.stack([b_own, b_far])
    c_pair = jnp.stack([c_own, c_side])
    b_pair_side = swap_y(b_pair)
    c_pair_far = swap_x(c_pair)

    def gather_z(own, gate):
        seen, parts = own, []
        for i, k in enumerate(outer_bits()):
            got = swap(after(seen, gate) if i == 0 else seen, "tok", 1 << k)
            parts.append(got)
            seen = jnp.concatenate([seen, got], axis=0)
        return jnp.concatenate(parts, axis=0)

    b_rest = gather_z(b_own, marks[0])
    c_rest = gather_z(c_own, marks[-1])

    h1_y = swap_y(a_seen[0])
    h2_x = swap_x(a_seen[1])
    h1_near = jnp.concatenate([a_seen[0], h1_y], axis=0)
    h2_near = jnp.stack([a_seen[1], h2_x])
    h1_far = swap_x(h1_near)
    h2_y = swap_y(h2_near)
    h1 = jnp.concatenate([h1_near, h1_far], axis=1)
    h2 = jnp.concatenate([h2_near, h2_y], axis=1)
    h2 = jnp.concatenate([h2[0], h2[1]], axis=1)

    b_rest_far = swap_x(after(b_rest, h2_x))
    c_rest_side = swap_y(after(c_rest, h1_y))
    b_rest_pair = jnp.stack([b_rest, b_rest_far])
    c_rest_pair = jnp.stack([c_rest, c_rest_side])
    b_rest_pair_side = swap_y(after(b_rest_pair, h2_y))
    c_rest_pair_far = swap_x(after(c_rest_pair, h1_far))
    up = jnp.concatenate(
        [
            jnp.concatenate([b_pair[i], b_rest_pair[i], b_pair_side[i], b_rest_pair_side[i]], axis=0)
            for i in range(2)
        ],
        axis=1,
    )
    down = jnp.concatenate(
        [
            jnp.concatenate([c_pair[0], c_rest_pair[0], c_pair[1], c_rest_pair[1]], axis=0),
            jnp.concatenate(
                [c_pair_far[0], c_rest_pair_far[0], c_pair_far[1], c_rest_pair_far[1]], axis=0
            ),
        ],
        axis=1,
    )

    pair_small = jnp.stack([own_small.reshape(-1), far_small.reshape(-1)])
    qb = pair_small[:, 6 * local : 7 * local].reshape(2, 1, local)
    vb = pair_small[:, 7 * local : 8 * local].reshape(2, 1, local)
    upb = pair_small[:, 8 * local :].reshape(1, -1)
    wide = pair_small[:, : 6 * local].reshape(2, -1, 128)
    pieces = jnp.concatenate([wide, swap_core(wide)], axis=0).reshape(4, 6, local)
    pieces = pieces.transpose(1, 0, 2).reshape(6, dim)
    vectors = jnp.dot(pieces, order.astype(F32), precision=lax.Precision.HIGHEST)
    gain1, shift1, gain2, shift2, obias, dbias = [vectors[i : i + 1] for i in range(6)]

    values, normed1 = tokens(pair_in, other_in, select, order, gain1, shift1)
    (grads,) = tokens(pair_out, other_out, select, order)
    q, k, v, att, probs, mixed = attend(normed1, h1, h2, qb, vb)
    residual, normed2 = middle(values, mixed, swap_core(mixed), obias, gain2, shift2)

    seats, wide_hidden = normed2.shape[0], up.shape[1]
    hidden, slope = resident(
        hidden_kernel,
        [((seats, wide_hidden), BF), ((seats, wide_hidden), F32)],
        normed2,
        up,
        upb,
        name="hidden",
    )
    d_before_b, dn2, up_sum = resident(
        hidden_back_kernel,
        [((seats, wide_hidden), BF), ((seats, dim), BF), ((1, wide_hidden), F32)],
        grads,
        down,
        slope,
        up,
        scratch=[pltpu.VMEM((seats, dim), F32)],
        name="hidden_back",
    )
    dn2_other = swap_core(dn2)
    wide_cols = up.shape[1] // 2
    half = dim // 2
    gc_far = dot_tn(grads, hidden[:, wide_cols:]).astype(BF)
    gc_own = dot_tn(grads, hidden[:, :wide_cols]).astype(BF)
    gb_far = dot_tn(normed2[:, half:], d_before_b).astype(BF)
    gb_own = dot_tn(normed2[:, :half], d_before_b).astype(BF)
    down_out = dot_nt(hidden, down).astype(BF)
    down_other = swap_core(down_out)

    def scatter_x_first(own, far):
        total = add_rows(own, swap_x(far))
        kept, sent = total[:half], total[half:].astype(BF)
        return scatter_outer(add_rows(kept, swap_y(sent)))

    def scatter_y_first(own, far, split):
        total = add_rows(own, swap_y(far))
        kept, sent = split(total)
        return scatter_outer(add_rows(kept, swap_x(sent.astype(BF))))

    grad_down = scatter_x_first(gc_own, gc_far)
    grad_up = scatter_y_first(gb_own, gb_far, lambda t: (t[:, :wide_cols], t[:, wide_cols:]))

    def put_together(own, far):
        got = swap_x(far)
        low = jnp.where(x == 0, own, got).astype(F32)
        high = jnp.where(x == 0, got, own).astype(F32)
        return jnp.pad(low, ((0, shift_rows), (0, 0))) + jnp.pad(high, ((shift_rows, 0), (0, 0)))

    out_own, out_far = pack(
        output_kernel, (residual, down_out, down_other, dbias), order_back, select_back, False
    )
    block_output = put_together(out_own, out_far).astype(BF)

    d_resid, d_resid_b, sums2 = middle_back(residual, grads, dn2, dn2_other, gain2)
    dq, dk, dv, dn1, q_sum, v_sum = attend_back(d_resid_b, q, k, v, probs, h1, h2)
    dn1_other = swap_core(dn1)
    qk_own = jnp.concatenate([dot_tn(normed1, dq[0]), dot_tn(normed1, dk[0])], axis=1).astype(BF)
    qk_far = jnp.concatenate([dot_tn(normed1, dq[1]), dot_tn(normed1, dk[1])], axis=1).astype(BF)
    att_all = jnp.concatenate([att[0], att[1]], axis=1)

    def value_grads(cols):
        return jnp.concatenate(
            [dot_tn(normed1[:, cols], dv), dot_tn(d_resid_b[:, cols], att_all)], axis=1
        ).astype(BF)

    vo_far = value_grads(slice(half, dim))
    vo_own = value_grads(slice(0, half))
    grad_qk = scatter_x_first(qk_own, qk_far)

    def split_vo(total):
        cut = [total[:, i * local : (i + 1) * local] for i in range(4)]
        return jnp.concatenate([cut[0], cut[2]], axis=1), jnp.concatenate([cut[1], cut[3]], axis=1)

    grad_vo = scatter_y_first(vo_own, vo_far, split_vo)
    in_own, in_far, sums1 = pack(
        input_kernel, (d_resid, dn1, dn1_other, values, gain1), order_back, select_back, True
    )
    input_grad = put_together(in_own, in_far)

    vecs = jnp.concatenate([sums1[:2], sums2[:4]], axis=0)
    vecs = jnp.dot(vecs, order_back.astype(F32), precision=lax.Precision.HIGHEST)
    up_sum = up_sum[0]
    small = [
        jnp.concatenate(
            [vecs[:, i * local : (i + 1) * local].reshape(-1), q_sum[i, 0], v_sum[i, 0]]
            + [up_sum[i * wide_cols : (i + 1) * wide_cols]]
        ).reshape(-1, 128)
        for i in range(2)
    ]
    total = small[0] + swap_x(small[1])
    for i in range(bits):
        total = total + swap(total, "tok", 1 << i)
    total = total.reshape(-1)
    cut = lambda i: total[i * local : (i + 1) * local]

    return (
        block_output,
        input_grad,
        cut(0),
        cut(1),
        jnp.concatenate([grad_qk, grad_vo[:, :local]], axis=1).reshape(qkv_weight.shape),
        cut(6),
        cut(7),
        grad_vo[:, local:].T,
        cut(4),
        cut(2),
        cut(3),
        grad_up,
        total[8 * local :],
        grad_down.T,
        cut(5),
    )


def solution(mesh):
    vec = P("feat")
    act = P("tok", "feat")
    qkv = P("tok", None, "feat")
    turned = P("feat", "tok")
    in_specs = (act, vec, vec, qkv, vec, vec, turned, vec, vec, vec, act, vec, turned, vec, act)
    out_specs = (act, act, vec, vec, qkv, vec, vec, turned, vec, vec, vec, act, vec, turned, vec)
    return jax.shard_map(body, mesh=mesh, in_specs=in_specs, out_specs=out_specs, check_vma=False)
```
